256 devices in a mesh: tile: 64 (over x, z, core), rep: 4 (over y).
Axes of the slice: x: 4, y: 4, z: 8, core: 2. Of those that a mesh axis runs over, the one named last changes fastest.
Arguments:
- sequence_codes: int32 [41472], replicated, may hold values from 0 to 3
- pair_allowed: int32 [32768, 512], P('tile', 'rep'), may hold values 0 or 1
- stack_weight: float32 [4, 4], replicated, may hold values from 0.3 to 3
- hairpin_weight: float32 [4, 4], replicated, may hold values from 0.5 to 5
- loop_weight: float32 [31, 31], replicated, may hold values from 0.0005 to 0.01
- inner_pairs: float32 [32768, 542], P('tile'), may hold values from 0.1 to 10
- multi_left: float32 [32768, 16, 512], P('tile', None, 'rep'), may hold values from 0.1 to 10
- branch_right: float32 [64, 16, 512, 512], P('tile', None, 'rep'), may hold values from 1.2207031e-05 to 0.0012207031
Outputs:
- paired_window: float32 [32768, 512], P('tile', 'rep')
- multi_split: float32 [32768, 512], P('tile', 'rep')
The draws below stay inside these ranges and needn't reach their ends.
All inputs are finite; a program needn't handle non-finite values. No bound on the sum of `pair_allowed` on one device may be relied on, other than what follows from the above.
Results may differ from the reference program's by a relative error of at most 0.0003.
Values sent between devices are 32-bit elements; how exact they have to be, the bound alone decides.
A program may use at most 192 MiB of HBM per device.

```python
import math
import jax
import jax.numpy as jnp
from jax import lax

TILE_LEN = 512
SPANS = 512
LOOP = 30
PANELS = 16
SPAN = 8192
POSITIONS = 32768
CODES_LEN = 41472
TILES = 64
N_TILE = 64


def set_ends(entries, key, smallest, high):
    index_at = [jax.random.randint(jax.random.fold_in(key, axis), (), 0, length) for axis, length in enumerate(entries.shape)]
    main_axis = entries.shape.index(max(entries.shape))
    neighbour = index_at[:main_axis] + [(index_at[main_axis] + 1) % entries.shape[main_axis]] + index_at[main_axis + 1:]
    return entries.at[tuple(index_at)].set(smallest).at[tuple(neighbour)].set(high)


def levels(key, dims, shards, low, top_value):
    level = 1.0
    for dim, parts in shards:
        heights = jax.random.uniform(jax.random.fold_in(jax.random.fold_in(key, 6), dim), (parts,), jnp.float32, low / len(shards), top_value / len(shards))
        level = level * jnp.repeat(jnp.exp(heights), dims[dim] // parts).reshape((-1,) + (1,) * (len(dims) - 1 - dim))
    return level


def setup_inputs(seed: int = 0) -> dict:
    keys = jax.random.split(jax.random.key(seed), 9)
    sequence_codes = set_ends(jax.random.randint(keys[0], (CODES_LEN,), 0, 4), jax.random.fold_in(keys[0], 1), 0, 3).astype(jnp.int32)
    pair_allowed = set_ends((jax.random.randint(keys[1], (POSITIONS, SPANS), 0, 4) < 3).astype(jnp.int32), jax.random.fold_in(keys[1], 1), 0, 1)
    stack_weight = jnp.clip(jnp.exp(jax.random.uniform(keys[2], (4, 4), jnp.float32, math.log(0.3), math.log(3.0))), 0.3, 3.0)
    hairpin_weight = jnp.clip(jnp.exp(jax.random.uniform(keys[3], (4, 4), jnp.float32, math.log(0.5), math.log(5.0))), 0.5, 5.0)
    loop_weight = jnp.clip(jnp.exp(jax.random.uniform(keys[4], (LOOP + 1, LOOP + 1), jnp.float32, math.log(0.0005), math.log(0.01))), 0.0005, 0.01)
    inner_pairs = jnp.clip(jnp.exp(math.log(10.0) - 4.6051702 * jax.random.uniform(keys[5], (POSITIONS, SPANS + LOOP), jnp.float32) ** levels(keys[5], (POSITIONS, SPANS + LOOP), ((0, 64),), -0.2, 0.2)), 0.1, 10.0)
    multi_left = jnp.clip(jnp.exp(math.log(10.0) - 4.6051702 * jax.random.uniform(keys[6], (POSITIONS, PANELS, TILE_LEN), jnp.float32) ** levels(keys[6], (POSITIONS, PANELS, TILE_LEN), ((0, 64), (2, 4)), -0.2, 0.2)), 0.1, 10.0)
    branch_right = jnp.clip(jnp.exp(math.log(0.0012207031) - 4.6051702 * jax.random.uniform(keys[7], (TILES, PANELS, TILE_LEN, TILE_LEN), jnp.float32) ** levels(keys[7], (TILES, PANELS, TILE_LEN, TILE_LEN), ((0, 64), (2, 4)), -0.2, 0.2)), 1.220703143189894e-05, 0.0012207031)
    return dict(sequence_codes=sequence_codes, pair_allowed=pair_allowed, stack_weight=stack_weight, hairpin_weight=hairpin_weight, loop_weight=loop_weight, inner_pairs=inner_pairs, multi_left=multi_left, branch_right=branch_right)


def band_matrix(weights, offset, width):
    source = jnp.arange(width + LOOP, dtype=jnp.int32)[:, None]
    target = jnp.arange(width, dtype=jnp.int32)[None, :]
    right_len = target + LOOP + 2 - offset - source
    inside = (right_len >= 1) & (right_len <= LOOP + 2 - offset)
    values = jnp.take(weights, jnp.clip(right_len - 1, 0, LOOP))
    return jnp.where(inside, values, jnp.zeros_like(values))


def reference(sequence_codes, pair_allowed, stack_weight, hairpin_weight, loop_weight, inner_pairs, multi_left, branch_right):
    extended = jnp.concatenate([inner_pairs, jnp.zeros((LOOP + 1, SPANS + LOOP), inner_pairs.dtype)], 0)

    def add_offset(running, offset):
        shifted = lax.dynamic_slice_in_dim(extended, offset, POSITIONS, 0)
        weights = lax.dynamic_index_in_dim(loop_weight, offset - 1, 0, keepdims=False)
        band_values = band_matrix(weights, offset, SPANS)
        return running + jnp.dot(shifted, band_values, precision=lax.Precision.HIGHEST), None

    interior, _ = lax.scan(add_offset, jnp.zeros((POSITIONS, SPANS), inner_pairs.dtype), jnp.arange(1, LOOP + 2, dtype=jnp.int32))
    row_pos = jnp.arange(POSITIONS, dtype=jnp.int32)
    five_prime = sequence_codes[:POSITIONS]
    pair_index = row_pos[:, None] + SPAN + jnp.arange(SPANS, dtype=jnp.int32)[None, :]
    three_prime = sequence_codes[pair_index]
    stack_vals = stack_weight[five_prime[:, None], three_prime]
    hairpin_vals = hairpin_weight[five_prime[:, None], three_prime]
    paired_window = (pair_allowed.astype(inner_pairs.dtype) * stack_vals) * (hairpin_vals + interior)

    def tile_term(tile_id):
        left_part = lax.dynamic_slice_in_dim(multi_left, tile_id * TILE_LEN, TILE_LEN, 0)
        local_row = jnp.arange(TILE_LEN, dtype=jnp.int32)[:, None]
        split_pos = jnp.arange(TILE_LEN, dtype=jnp.int32)[None, :]
        first_panel = jnp.where(split_pos > local_row, left_part[:, 0, :], jnp.zeros_like(left_part[:, 0, :]))
        left_part = left_part.at[:, 0, :].set(first_panel)
        panel_ids = jnp.arange(PANELS, dtype=jnp.int32)
        sources = (tile_id + panel_ids) % N_TILE
        right_part = branch_right[sources, panel_ids]
        return jnp.einsum("xmw,mwc->xc", left_part, right_part, precision=lax.Precision.HIGHEST)

    multi_split = lax.map(tile_term, jnp.arange(N_TILE, dtype=jnp.int32)).reshape(POSITIONS, TILE_LEN)
    return paired_window, multi_split
```

```python
import functools

import jax
import jax.numpy as jnp
from jax import lax
from jax.experimental import pallas as pl
from jax.experimental.pallas import tpu as pltpu
from jax.sharding import PartitionSpec as P

LOOP = 30
SPAN = 8192
LANES = 128
RIM = 32
MESH = pl.DeviceIdType.MESH
F32 = jnp.float32
BF16 = jnp.bfloat16
BLOCK_ORDER = (2, 1, 3, 0)


def halves(value):
    high = value.astype(BF16)
    return high, (value - high.astype(F32)).astype(BF16)


def dot(left, right):
    return jnp.dot(left, right, preferred_element_type=F32)


def product(left_high, left_low, right):
    right_high, right_low = halves(right)
    width = right.shape[1]
    both = dot(left_high, jnp.concatenate([right_high, right_low], 1))
    return both[:, :width] + both[:, width:] + dot(left_low, right_high)


def kernel(
    tiles,
    reps,
    stack_ref,
    hairpin_ref,
    loop_ref,
    codes_hbm,
    allowed_hbm,
    inner_hbm,
    left_hbm,
    right_hbm,
    paired_hbm,
    split_hbm,
    codes,
    allowed,
    inner,
    rows,
    moving,
    weights,
    interior,
    left,
    left_high,
    left_low,
    panels,
    sums,
    others,
    local_sem,
    panel_send,
    panel_recv,
    rim_send,
    rim_recv,
    sum_send,
    sum_recv,
):
    tile = lax.axis_index("tile")
    rep = lax.axis_index("rep")
    panel_count, depth, _ = panels.shape
    row_count = rows.shape[0] - RIM

    def tile_at(step):
        return lax.rem(tile + step + tiles, tiles)

    def rep_at(step):
        return lax.rem(rep + step + reps, reps)

    barrier = pltpu.get_barrier_semaphore()

    @pl.loop(1, panel_count)
    def _(distance):
        pl.semaphore_signal(
            barrier, inc=1, device_id={"tile": tile_at(distance)}, device_id_type=MESH
        )

    for step in range(1, reps):
        pl.semaphore_signal(barrier, inc=1, device_id={"rep": rep_at(step)}, device_id_type=MESH)

    fetch_inner = pltpu.make_async_copy(inner_hbm, inner, local_sem.at[0])
    fetch_left = pltpu.make_async_copy(left_hbm, left, local_sem.at[1])
    fetch_right = pltpu.make_async_copy(right_hbm.at[0], panels.at[0], local_sem.at[2])
    fetch_codes = pltpu.make_async_copy(codes_hbm, codes, local_sem.at[3])
    fetch_allowed = pltpu.make_async_copy(allowed_hbm, allowed, local_sem.at[4])
    fetch_inner.start()
    fetch_left.start()
    fetch_right.start()
    fetch_codes.start()
    fetch_allowed.start()
    pl.semaphore_wait(barrier, panel_count - 1 + reps - 1)

    def columns(block):
        start = rep_at(BLOCK_ORDER[block]) * LANES
        return pl.ds(pl.multiple_of(start, LANES), LANES)

    def panel_copy(distance, block):
        place = (distance, slice(None), columns(block))
        return pltpu.make_async_remote_copy(
            src_ref=right_hbm.at[place],
            dst_ref=panels.at[place],
            send_sem=panel_send.at[distance, block],
            recv_sem=panel_recv.at[distance, block],
            device_id={"tile": tile_at(-distance)},
            device_id_type=MESH,
        )

    def send_block(block):
        @pl.loop(1, panel_count)
        def _(distance):
            panel_copy(distance, block).start()

    send_block(0)

    fetch_inner.wait()
    main_part = inner[pl.ds(pl.multiple_of(rep * LANES, LANES), LANES), :]
    rows[0:row_count, 0:LANES] = main_part.T
    tail_part = inner[pl.ds(pl.multiple_of((rep + 1) * LANES - 8, 8), LOOP + 8), :]
    rows[0:row_count, LANES : 2 * LANES] = jnp.zeros((row_count, LANES), F32)
    rows[0:row_count, LANES : LANES + LOOP + 8] = tail_part.T

    fetch_left.wait()
    own_row = lax.broadcasted_iota(jnp.int32, (row_count, LANES), 0)
    own_lane = lax.broadcasted_iota(jnp.int32, (row_count, LANES), 1)
    for panel in range(panel_count):
        value = left[pl.ds(panel, row_count, stride=panel_count), :]
        if panel == 0:
            value = jnp.where(own_lane + rep * LANES > own_row, value, 0.0)
        high, low = halves(value)
        at = slice((panel % 2) * LANES, (panel % 2 + 1) * LANES)
        left_high[panel // 2, :, at] = high
        left_low[panel // 2, :, at] = low

    rim_copy = pltpu.make_async_remote_copy(
        src_ref=rows.at[0:RIM],
        dst_ref=rows.at[row_count : row_count + RIM],
        send_sem=rim_send,
        recv_sem=rim_recv,
        device_id={"tile": tile_at(-1)},
        device_id_type=MESH,
    )
    rim_copy.start()
    for block in range(1, reps):
        send_block(block)
    fetch_right.wait()

    def add_pair(block, pair):
        @pl.when(pair > 0)
        def _():
            panel_copy(2 * pair, block).wait_recv()

        panel_copy(2 * pair + 1, block).wait_recv()
        right = panels[pl.ds(2 * pair, 2), :, columns(block)].reshape(2 * depth, LANES)
        value = product(left_high[pair], left_low[pair], right)

        @pl.when(pair == 0)
        def _():
            sums[block] = value

        @pl.when(pair > 0)
        def _():
            sums[block] += value

    def sum_copy(block):
        step = BLOCK_ORDER[block]
        return pltpu.make_async_remote_copy(
            src_ref=sums.at[block],
            dst_ref=others.at[block],
            send_sem=sum_send.at[block],
            recv_sem=sum_recv.at[block],
            device_id={"rep": rep_at(step)},
            device_id_type=MESH,
        )

    def work_block(block, first):
        @pl.loop(first, panel_count // 2)
        def _(pair):
            add_pair(block, pair)

    work_block(0, 0)

    rim_copy.wait_recv()

    @pl.when(tile == tiles - 1)
    def _():
        rows[row_count : row_count + RIM, :] = jnp.zeros((RIM, 2 * LANES), F32)

    sum_copy(0).start()
    weights[...] = jnp.zeros_like(weights)
    weights[0 : LOOP + 1, 0 : LOOP + 1] = loop_ref[...]
    interior[...] = jnp.zeros_like(interior)

    moving[...] = rows[...]

    def staircase(row, direction):
        width = row.shape[1]
        step = jnp.broadcast_to(row, (8, width))
        down = lax.broadcasted_iota(jnp.int32, (8, width), 0)
        for bit in (1, 2, 4):
            step = jnp.where(down & bit != 0, pltpu.roll(step, (direction * bit) % width, 1), step)
        return step

    tall = (LANES + 40, LANES)
    source = lax.broadcasted_iota(jnp.int32, tall, 0)
    source = jnp.where(source < LANES, source, source - 8)
    behind = source - lax.broadcasted_iota(jnp.int32, tall, 1)
    behind = jnp.where(lax.broadcasted_iota(jnp.int32, tall, 0) // 8 == LANES // 8, -1, behind)
    groups = [group % 16 for group in (*range(16), *range(15, 20))]

    @pl.loop(1, LOOP + 2)
    def _(offset):
        row = pltpu.roll(weights[pl.ds(offset - 1, 1), :], LANES - LOOP - 1 + offset, 1)
        step = staircase(row, 1)
        bands = jnp.concatenate([pltpu.roll(step, 8 * group, 1) for group in groups], 0)
        bands = jnp.where((behind >= 0) & (behind <= LOOP + 1 - offset), bands, 0.0)
        bands = jnp.concatenate([bands, jnp.zeros((LANES - 40, LANES), F32)], 0)
        later = moving[1 : row_count + RIM, :]
        moving[0 : row_count + RIM - 1, :] = later
        high, low = halves(later[0:row_count])
        interior[...] += product(high, low, bands)

    fetch_codes.wait()
    fetch_allowed.wait()
    row_blocks = row_count // LANES
    square = (LANES, LANES)
    down = lax.broadcasted_iota(jnp.int32, square, 0)
    across = lax.broadcasted_iota(jnp.int32, square, 1)
    ones = jnp.ones(square, BF16)
    code_row = tile * row_blocks
    for part in range(row_blocks):
        five = codes[pl.ds(code_row + part, 1), :]
        five = jnp.where(down == across, jnp.broadcast_to(five, square), 0).astype(F32)
        three_row = code_row + SPAN // LANES + rep + part
        three = jnp.concatenate(
            [codes[pl.ds(three_row, 1), :], codes[pl.ds(three_row + 1, 1), :]], 1
        ).astype(F32)
        step = staircase(three, -1)
        three = jnp.concatenate(
            [pltpu.roll(step, (-8 * group) % (2 * LANES), 1)[:, :LANES] for group in range(16)], 0
        )
        code = dot((4.0 * five).astype(BF16), ones) + three
        stack_value = jnp.zeros(square, F32)
        hairpin_value = jnp.zeros(square, F32)
        for first in range(4):
            for second in range(4):
                match = code == float(4 * first + second)
                stack_value = jnp.where(match, stack_ref[first, second], stack_value)
                hairpin_value = jnp.where(match, hairpin_ref[first, second], hairpin_value)
        at = slice(part * LANES, (part + 1) * LANES)
        interior[at] = (allowed[at].astype(F32) * stack_value) * (hairpin_value + interior[at])

    for block in range(1, reps):
        work_block(block, 0) if block < reps - 1 else None
        if block == 1:
            store_paired = pltpu.make_async_copy(interior, paired_hbm, local_sem.at[5])
            store_paired.start()
        if block < reps - 1:
            sum_copy(block).start()
    work_block(reps - 1, 0)

    for block in range(reps - 1):
        sum_copy(block).wait_recv()
    sums[reps - 1] = (sums[reps - 1] + others[0]) + (others[1] + others[2])
    store_split = pltpu.make_async_copy(sums.at[reps - 1], split_hbm, local_sem.at[6])
    store_split.start()
    store_paired.wait()
    store_split.wait()
    rim_copy.wait_send()
    for block in range(reps):

        @pl.loop(1, panel_count)
        def _(distance):
            panel_copy(distance, block).wait_send()

        if block < reps - 1:
            sum_copy(block).wait_send()


def on_device(
    tiles,
    reps,
    sequence_codes,
    pair_allowed,
    stack_weight,
    hairpin_weight,
    loop_weight,
    inner_pairs,
    multi_left,
    branch_right,
):
    row_count, cols_local = pair_allowed.shape
    panel_count = multi_left.shape[1]
    codes = sequence_codes.reshape(-1, LANES)
    inner = inner_pairs.T
    left = multi_left.reshape(row_count * panel_count, cols_local)
    right = branch_right[0]
    out = jax.ShapeDtypeStruct((row_count, cols_local), F32)
    any_space = pl.BlockSpec(memory_space=pl.ANY)
    smem = pl.BlockSpec(memory_space=pltpu.SMEM)
    vmem = pl.BlockSpec(memory_space=pltpu.VMEM)
    block = (row_count, LANES)
    pairs = (panel_count // 2, row_count, 2 * LANES)
    dma = pltpu.SemaphoreType.DMA
    return pl.pallas_call(
        functools.partial(kernel, tiles, reps),
        out_shape=(out, out),
        in_specs=[smem, smem, vmem] + [any_space] * 5,
        out_specs=(any_space, any_space),
        scratch_shapes=[
            pltpu.VMEM(codes.shape, jnp.int32),
            pltpu.VMEM(block, jnp.int32),
            pltpu.VMEM(inner.shape, F32),
            pltpu.VMEM((row_count + RIM, 2 * LANES), F32),
            pltpu.VMEM((row_count + RIM, 2 * LANES), F32),
            pltpu.VMEM((32, LANES), F32),
            pltpu.VMEM(block, F32),
            pltpu.VMEM(left.shape, F32),
            pltpu.VMEM(pairs, BF16),
            pltpu.VMEM(pairs, BF16),
            pltpu.VMEM(right.shape, F32),
            pltpu.VMEM((reps,) + block, F32),
            pltpu.VMEM((reps - 1,) + block, F32),
            dma((7,)),
            dma((panel_count, reps)),
            dma((panel_count, reps)),
            dma,
            dma,
            dma((reps - 1,)),
            dma((reps - 1,)),
        ],
        compiler_params=pltpu.CompilerParams(
            collective_id=0, has_side_effects=True, vmem_limit_bytes=60 << 20
        ),
    )(stack_weight, hairpin_weight, loop_weight, codes, pair_allowed, inner, left, right)


def solution(mesh):
    placed = (
        P(),
        P("tile", "rep"),
        P(),
        P(),
        P(),
        P("tile", None),
        P("tile", None, "rep"),
        P("tile", None, "rep", None),
    )
    return jax.shard_map(
        functools.partial(on_device, mesh.shape["tile"], mesh.shape["rep"]),
        mesh=mesh,
        in_specs=placed,
        out_specs=(P("tile", "rep"), P("tile", "rep")),
        check_vma=False,
    )
```

```python
import functools

import jax
import jax.numpy as jnp
from jax import lax
from jax.experimental import pallas as pl
from jax.experimental.pallas import tpu as pltpu
from jax.sharding import PartitionSpec as P

LOOP = 30
SPAN = 8192
LANES = 128
RIM = 32
MESH = pl.DeviceIdType.MESH
F32 = jnp.float32
BF16 = jnp.bfloat16
BLOCK_ORDER = (2, 1, 3, 0)
SEND_ORDER = (2, 14, 4, 12, 6, 10, 8, 1, 15, 3, 13, 5, 11, 7, 9)


def halves(value):
    high = value.astype(BF16)
    return high, (value - high.astype(F32)).astype(BF16)


def dot(left, right):
    return jnp.dot(left, right, preferred_element_type=F32)


def product(left_high, left_low, right):
    right_high, right_low = halves(right)
    width = right.shape[1]
    both = dot(left_high, jnp.concatenate([right_high, right_low], 1))
    return both[:, :width] + both[:, width:] + dot(left_low, right_high)


def kernel(
    tiles,
    reps,
    stack_ref,
    hairpin_ref,
    loop_ref,
    codes_hbm,
    allowed_hbm,
    inner_hbm,
    left_hbm,
    right_hbm,
    paired_hbm,
    split_hbm,
    codes,
    allowed,
    inner,
    rows,
    moving,
    weights,
    interior,
    left,
    left_high,
    left_low,
    panels,
    sums,
    others,
    local_sem,
    panel_send,
    panel_recv,
    rim_send,
    rim_recv,
    sum_send,
    sum_recv,
):
    tile = lax.axis_index("tile")
    rep = lax.axis_index("rep")
    panel_count, depth, _ = panels.shape
    row_count = rows.shape[0] - RIM

    def tile_at(step):
        return lax.rem(tile + step + tiles, tiles)

    def rep_at(step):
        return lax.rem(rep + step + reps, reps)

    barrier = pltpu.get_barrier_semaphore()

    @pl.loop(1, panel_count)
    def _(distance):
        pl.semaphore_signal(
            barrier, inc=1, device_id={"tile": tile_at(distance)}, device_id_type=MESH
        )

    for step in range(1, reps):
        pl.semaphore_signal(barrier, inc=1, device_id={"rep": rep_at(step)}, device_id_type=MESH)

    fetch_inner = pltpu.make_async_copy(inner_hbm, inner, local_sem.at[0])
    fetch_left = pltpu.make_async_copy(left_hbm, left, local_sem.at[1])
    fetch_right = pltpu.make_async_copy(right_hbm.at[0], panels.at[0], local_sem.at[2])
    fetch_codes = pltpu.make_async_copy(codes_hbm, codes, local_sem.at[3])
    fetch_allowed = pltpu.make_async_copy(allowed_hbm, allowed, local_sem.at[4])
    fetch_inner.start()
    fetch_left.start()
    fetch_right.start()
    fetch_codes.start()
    fetch_allowed.start()
    pl.semaphore_wait(barrier, panel_count - 1 + reps - 1)

    def columns(block):
        start = rep_at(BLOCK_ORDER[block]) * LANES
        return pl.ds(pl.multiple_of(start, LANES), LANES)

    def panel_copy(distance, block):
        place = (distance, slice(None), columns(block))
        return pltpu.make_async_remote_copy(
            src_ref=right_hbm.at[place],
            dst_ref=panels.at[place],
            send_sem=panel_send,
            recv_sem=panel_recv.at[distance // 2, block],
            device_id={"tile": tile_at(-distance)},
            device_id_type=MESH,
        )

    def send_block(block):
        for distance in SEND_ORDER if block < reps - 1 else range(1, panel_count):
            panel_copy(distance, block).start()

    send_block(0)

    fetch_inner.wait()
    main_part = inner[pl.ds(pl.multiple_of(rep * LANES, LANES), LANES), :]
    rows[0:row_count, 0:LANES] = main_part.T
    tail_part = inner[pl.ds(pl.multiple_of((rep + 1) * LANES - 8, 8), LOOP + 8), :]
    rows[0:row_count, LANES : 2 * LANES] = jnp.zeros((row_count, LANES), F32)
    rows[0:row_count, LANES : LANES + LOOP + 8] = tail_part.T

    fetch_left.wait()
    own_row = lax.broadcasted_iota(jnp.int32, (row_count, LANES), 0)
    own_lane = lax.broadcasted_iota(jnp.int32, (row_count, LANES), 1)
    for panel in range(panel_count):
        value = left[pl.ds(panel, row_count, stride=panel_count), :]
        if panel == 0:
            value = jnp.where(own_lane + rep * LANES > own_row, value, 0.0)
        high, low = halves(value)
        at = slice((panel % 2) * LANES, (panel % 2 + 1) * LANES)
        left_high[panel // 2, :, at] = high
        left_low[panel // 2, :, at] = low

    rim_copy = pltpu.make_async_remote_copy(
        src_ref=rows.at[0:RIM],
        dst_ref=rows.at[row_count : row_count + RIM],
        send_sem=rim_send,
        recv_sem=rim_recv,
        device_id={"tile": tile_at(-1)},
        device_id_type=MESH,
    )
    rim_copy.start()
    for block in range(1, reps):
        send_block(block)
    fetch_right.wait()

    def wait_for(first, count, place, sem):
        ref = panels.at[pl.ds(first, count), :, place]
        pltpu.make_async_copy(ref, ref, sem).wait()

    def add_pair(block, pair):
        @pl.when(pair > 0)
        def _():
            wait_for(2 * pair, 2, columns(block), panel_recv.at[pair, block])

        @pl.when(pair == 0)
        def _():
            wait_for(1, 1, columns(block), panel_recv.at[pair, block])

        right = panels[pl.ds(2 * pair, 2), :, columns(block)].reshape(2 * depth, LANES)
        value = product(left_high[pair], left_low[pair], right)

        @pl.when(pair == 0)
        def _():
            sums[block] = value

        @pl.when(pair > 0)
        def _():
            sums[block] += value

    def sum_copy(block):
        step = BLOCK_ORDER[block]
        return pltpu.make_async_remote_copy(
            src_ref=sums.at[block],
            dst_ref=others.at[block],
            send_sem=sum_send,
            recv_sem=sum_recv.at[block],
            device_id={"rep": rep_at(step)},
            device_id_type=MESH,
        )

    def work_block(block, first):
        @pl.loop(first, panel_count // 2)
        def _(pair):
            add_pair(block, pair)

    work_block(0, 0)

    rim_copy.wait_recv()

    @pl.when(tile == tiles - 1)
    def _():
        rows[row_count : row_count + RIM, :] = jnp.zeros((RIM, 2 * LANES), F32)

    sum_copy(0).start()
    weights[...] = jnp.zeros_like(weights)
    weights[0 : LOOP + 1, 0 : LOOP + 1] = loop_ref[...]
    interior[...] = jnp.zeros_like(interior)

    moving[...] = rows[...]

    def staircase(row, direction):
        width = row.shape[1]
        step = jnp.broadcast_to(row, (8, width))
        down = lax.broadcasted_iota(jnp.int32, (8, width), 0)
        for bit in (1, 2, 4):
            step = jnp.where(down & bit != 0, pltpu.roll(step, (direction * bit) % width, 1), step)
        return step

    tall = (LANES + 40, LANES)
    source = lax.broadcasted_iota(jnp.int32, tall, 0)
    source = jnp.where(source < LANES, source, source - 8)
    behind = source - lax.broadcasted_iota(jnp.int32, tall, 1)
    behind = jnp.where(lax.broadcasted_iota(jnp.int32, tall, 0) // 8 == LANES // 8, -1, behind)
    groups = [group % 16 for group in (*range(16), *range(15, 20))]

    @pl.loop(1, LOOP + 2)
    def _(offset):
        row = pltpu.roll(weights[pl.ds(offset - 1, 1), :], LANES - LOOP - 1 + offset, 1)
        step = staircase(row, 1)
        bands = jnp.concatenate([pltpu.roll(step, 8 * group, 1) for group in groups], 0)
        bands = jnp.where((behind >= 0) & (behind <= LOOP + 1 - offset), bands, 0.0)
        bands = jnp.concatenate([bands, jnp.zeros((LANES - 40, LANES), F32)], 0)
        later = moving[1 : row_count + RIM, :]
        moving[0 : row_count + RIM - 1, :] = later
        high, low = halves(later[0:row_count])
        interior[...] += product(high, low, bands)

    fetch_codes.wait()
    fetch_allowed.wait()
    row_blocks = row_count // LANES
    square = (LANES, LANES)
    down = lax.broadcasted_iota(jnp.int32, square, 0)
    across = lax.broadcasted_iota(jnp.int32, square, 1)
    ones = jnp.ones(square, BF16)
    code_row = tile * row_blocks
    for part in range(row_blocks):
        five = codes[pl.ds(code_row + part, 1), :]
        five = jnp.where(down == across, jnp.broadcast_to(five, square), 0).astype(F32)
        three_row = code_row + SPAN // LANES + rep + part
        three = jnp.concatenate(
            [codes[pl.ds(three_row, 1), :], codes[pl.ds(three_row + 1, 1), :]], 1
        ).astype(F32)
        step = staircase(three, -1)
        three = jnp.concatenate(
            [pltpu.roll(step, (-8 * group) % (2 * LANES), 1)[:, :LANES] for group in range(16)], 0
        )
        code = dot((4.0 * five).astype(BF16), ones) + three
        stack_value = jnp.zeros(square, F32)
        hairpin_value = jnp.zeros(square, F32)
        for first in range(4):
            for second in range(4):
                match = code == float(4 * first + second)
                stack_value = jnp.where(match, stack_ref[first, second], stack_value)
                hairpin_value = jnp.where(match, hairpin_ref[first, second], hairpin_value)
        at = slice(part * LANES, (part + 1) * LANES)
        interior[at] = (allowed[at].astype(F32) * stack_value) * (hairpin_value + interior[at])

    for block in range(1, reps):
        work_block(block, 0) if block < reps - 1 else None
        if block == 1:
            store_paired = pltpu.make_async_copy(interior, paired_hbm, local_sem.at[5])
            store_paired.start()
        if block < reps - 1:
            sum_copy(block).start()
    work_block(reps - 1, 0)

    for block in range(reps - 1):
        sum_copy(block).wait_recv()
    sums[reps - 1] = (sums[reps - 1] + others[0]) + (others[1] + others[2])
    store_split = pltpu.make_async_copy(sums.at[reps - 1], split_hbm, local_sem.at[6])
    store_split.start()
    store_paired.wait()
    store_split.wait()
    rim_copy.wait_send()
    wait_for(1, panel_count - 1, slice(None), panel_send)
    sent = sums.at[0 : reps - 1]
    pltpu.make_async_copy(sent, sent, sum_send).wait()


def on_device(
    tiles,
    reps,
    sequence_codes,
    pair_allowed,
    stack_weight,
    hairpin_weight,
    loop_weight,
    inner_pairs,
    multi_left,
    branch_right,
):
    row_count, cols_local = pair_allowed.shape
    panel_count = multi_left.shape[1]
    codes = sequence_codes.reshape(-1, LANES)
    inner = inner_pairs.T
    left = multi_left.reshape(row_count * panel_count, cols_local)
    right = branch_right[0]
    out = jax.ShapeDtypeStruct((row_count, cols_local), F32)
    any_space = pl.BlockSpec(memory_space=pl.ANY)
    smem = pl.BlockSpec(memory_space=pltpu.SMEM)
    vmem = pl.BlockSpec(memory_space=pltpu.VMEM)
    block = (row_count, LANES)
    pairs = (panel_count // 2, row_count, 2 * LANES)
    dma = pltpu.SemaphoreType.DMA
    return pl.pallas_call(
        functools.partial(kernel, tiles, reps),
        out_shape=(out, out),
        in_specs=[smem, smem, vmem] + [any_space] * 5,
        out_specs=(any_space, any_space),
        scratch_shapes=[
            pltpu.VMEM(codes.shape, jnp.int32),
            pltpu.VMEM(block, jnp.int32),
            pltpu.VMEM(inner.shape, F32),
            pltpu.VMEM((row_count + RIM, 2 * LANES), F32),
            pltpu.VMEM((row_count + RIM, 2 * LANES), F32),
            pltpu.VMEM((32, LANES), F32),
            pltpu.VMEM(block, F32),
            pltpu.VMEM(left.shape, F32),
            pltpu.VMEM(pairs, BF16),
            pltpu.VMEM(pairs, BF16),
            pltpu.VMEM(right.shape, F32),
            pltpu.VMEM((reps,) + block, F32),
            pltpu.VMEM((reps - 1,) + block, F32),
            dma((7,)),
            dma,
            dma((panel_count // 2, reps)),
            dma,
            dma,
            dma,
            dma((reps - 1,)),
        ],
        compiler_params=pltpu.CompilerParams(
            collective_id=0, has_side_effects=True, vmem_limit_bytes=60 << 20
        ),
    )(stack_weight, hairpin_weight, loop_weight, codes, pair_allowed, inner, left, right)


def solution(mesh):
    placed = (
        P(),
        P("tile", "rep"),
        P(),
        P(),
        P(),
        P("tile", None),
        P("tile", None, "rep"),
        P("tile", None, "rep", None),
    )
    return jax.shard_map(
        functools.partial(on_device, mesh.shape["tile"], mesh.shape["rep"]),
        mesh=mesh,
        in_specs=placed,
        out_specs=(P("tile", "rep"), P("tile", "rep")),
        check_vma=False,
    )
```

```python
import functools

import jax
import jax.numpy as jnp
from jax import lax
from jax.experimental import pallas as pl
from jax.experimental.pallas import tpu as pltpu
from jax.sharding import PartitionSpec as P

LOOP = 30
SPAN = 8192
LANES = 128
PIECES = 2
RIM = 32
MESH = pl.DeviceIdType.MESH
F32 = jnp.float32
BF16 = jnp.bfloat16
BLOCK_ORDER = (2, 1, 3, 0)
SEND_ORDER = (2, 14, 4, 12, 6, 10, 8, 1, 15, 3, 13, 5, 11, 7, 9)


def halves(value):
    high = value.astype(BF16)
    return high, (value - high.astype(F32)).astype(BF16)


def dot(left, right):
    return jnp.dot(left, right, preferred_element_type=F32)


def product(left_high, left_low, right):
    right_high, right_low = halves(right)
    width = right.shape[1]
    both = dot(left_high, jnp.concatenate([right_high, right_low], 1))
    return both[:, :width] + both[:, width:] + dot(left_low, right_high)


def kernel(
    tiles,
    reps,
    stack_ref,
    hairpin_ref,
    loop_ref,
    codes_hbm,
    allowed_hbm,
    inner_hbm,
    left_hbm,
    right_hbm,
    paired_hbm,
    split_hbm,
    codes,
    allowed,
    inner,
    rows,
    moving,
    weights,
    interior,
    left,
    left_high,
    left_low,
    panels,
    sums,
    others,
    local_sem,
    panel_send,
    panel_recv,
    rim_send,
    rim_recv,
    sum_send,
    sum_recv,
):
    tile = lax.axis_index("tile")
    rep = lax.axis_index("rep")
    panel_count, depth, _ = panels.shape
    row_count = rows.shape[0] - RIM

    def tile_at(step):
        return lax.rem(tile + step + tiles, tiles)

    def rep_at(step):
        return lax.rem(rep + step + reps, reps)

    barrier = pltpu.get_barrier_semaphore()

    @pl.loop(1, panel_count)
    def _(distance):
        pl.semaphore_signal(
            barrier, inc=1, device_id={"tile": tile_at(distance)}, device_id_type=MESH
        )

    for step in range(1, reps):
        pl.semaphore_signal(barrier, inc=1, device_id={"rep": rep_at(step)}, device_id_type=MESH)

    fetch_inner = pltpu.make_async_copy(inner_hbm, inner, local_sem.at[0])
    fetch_left = pltpu.make_async_copy(left_hbm, left, local_sem.at[1])
    fetch_right = pltpu.make_async_copy(right_hbm.at[0], panels.at[0], local_sem.at[2])
    fetch_codes = pltpu.make_async_copy(codes_hbm, codes, local_sem.at[3])
    fetch_allowed = pltpu.make_async_copy(allowed_hbm, allowed, local_sem.at[4])
    fetch_inner.start()
    fetch_left.start()
    fetch_right.start()
    fetch_codes.start()
    fetch_allowed.start()
    pl.semaphore_wait(barrier, panel_count - 1 + reps - 1)

    def columns(block):
        start = rep_at(BLOCK_ORDER[block]) * LANES
        return pl.ds(pl.multiple_of(start, LANES), LANES)

    def panel_copy(distance, block):
        place = (distance, slice(None), columns(block))
        return pltpu.make_async_remote_copy(
            src_ref=right_hbm.at[place],
            dst_ref=panels.at[place],
            send_sem=panel_send,
            recv_sem=panel_recv.at[distance // 2, block],
            device_id={"tile": tile_at(-distance)},
            device_id_type=MESH,
        )

    def send_block(block):
        for distance in SEND_ORDER if block < reps - 1 else range(1, panel_count):
            panel_copy(distance, block).start()

    send_block(0)

    fetch_inner.wait()
    main_part = inner[pl.ds(pl.multiple_of(rep * LANES, LANES), LANES), :]
    rows[0:row_count, 0:LANES] = main_part.T
    tail_part = inner[pl.ds(pl.multiple_of((rep + 1) * LANES - 8, 8), LOOP + 8), :]
    rows[0:row_count, LANES : 2 * LANES] = jnp.zeros((row_count, LANES), F32)
    rows[0:row_count, LANES : LANES + LOOP + 8] = tail_part.T

    fetch_left.wait()
    own_row = lax.broadcasted_iota(jnp.int32, (row_count, LANES), 0)
    own_lane = lax.broadcasted_iota(jnp.int32, (row_count, LANES), 1)
    for panel in range(panel_count):
        value = left[pl.ds(panel, row_count, stride=panel_count), :]
        if panel == 0:
            value = jnp.where(own_lane + rep * LANES > own_row, value, 0.0)
        high, low = halves(value)
        at = slice((panel % 2) * LANES, (panel % 2 + 1) * LANES)
        left_high[panel // 2, :, at] = high
        left_low[panel // 2, :, at] = low

    rim_copy = pltpu.make_async_remote_copy(
        src_ref=rows.at[0:RIM],
        dst_ref=rows.at[row_count : row_count + RIM],
        send_sem=rim_send,
        recv_sem=rim_recv,
        device_id={"tile": tile_at(-1)},
        device_id_type=MESH,
    )
    rim_copy.start()
    for block in range(1, reps):
        send_block(block)
    fetch_right.wait()

    def wait_for(first, count, place, sem):
        ref = panels.at[pl.ds(first, count), :, place]
        pltpu.make_async_copy(ref, ref, sem).wait()

    def add_pair(block, pair):
        @pl.when(pair > 0)
        def _():
            wait_for(2 * pair, 2, columns(block), panel_recv.at[pair, block])

        @pl.when(pair == 0)
        def _():
            wait_for(1, 1, columns(block), panel_recv.at[pair, block])

        right = panels[pl.ds(2 * pair, 2), :, columns(block)].reshape(2 * depth, LANES)
        value = product(left_high[pair], left_low[pair], right)

        @pl.when(pair == 0)
        def _():
            sums[block] = value

        @pl.when(pair > 0)
        def _():
            sums[block] += value

    def sum_copy(block):
        step = BLOCK_ORDER[block]
        return pltpu.make_async_remote_copy(
            src_ref=sums.at[block],
            dst_ref=others.at[block],
            send_sem=sum_send,
            recv_sem=sum_recv.at[block],
            device_id={"rep": rep_at(step)},
            device_id_type=MESH,
        )

    def work_block(block, first):
        @pl.loop(first, panel_count // 2)
        def _(pair):
            add_pair(block, pair)

    work_block(0, 0)

    rim_copy.wait_recv()

    @pl.when(tile == tiles - 1)
    def _():
        rows[row_count : row_count + RIM, :] = jnp.zeros((RIM, 2 * LANES), F32)

    sum_copy(0).start()
    weights[...] = jnp.zeros_like(weights)
    weights[0 : LOOP + 1, 0 : LOOP + 1] = loop_ref[...]
    interior[...] = jnp.zeros_like(interior)

    moving[...] = rows[...]

    def staircase(row, direction):
        width = row.shape[1]
        step = jnp.broadcast_to(row, (8, width))
        down = lax.broadcasted_iota(jnp.int32, (8, width), 0)
        for bit in (1, 2, 4):
            step = jnp.where(down & bit != 0, pltpu.roll(step, (direction * bit) % width, 1), step)
        return step

    tall = (LANES + 40, LANES)
    source = lax.broadcasted_iota(jnp.int32, tall, 0)
    source = jnp.where(source < LANES, source, source - 8)
    behind = source - lax.broadcasted_iota(jnp.int32, tall, 1)
    behind = jnp.where(lax.broadcasted_iota(jnp.int32, tall, 0) // 8 == LANES // 8, -1, behind)
    groups = [group % 16 for group in (*range(16), *range(15, 20))]

    @pl.loop(1, LOOP + 2)
    def _(offset):
        row = pltpu.roll(weights[pl.ds(offset - 1, 1), :], LANES - LOOP - 1 + offset, 1)
        step = staircase(row, 1)
        bands = jnp.concatenate([pltpu.roll(step, 8 * group, 1) for group in groups], 0)
        bands = jnp.where((behind >= 0) & (behind <= LOOP + 1 - offset), bands, 0.0)
        bands = jnp.concatenate([bands, jnp.zeros((LANES - 40, LANES), F32)], 0)
        later = moving[1 : row_count + RIM, :]
        moving[0 : row_count + RIM - 1, :] = later
        high, low = halves(later[0:row_count])
        interior[...] += product(high, low, bands)

    fetch_codes.wait()
    fetch_allowed.wait()
    row_blocks = row_count // LANES
    square = (LANES, LANES)
    down = lax.broadcasted_iota(jnp.int32, square, 0)
    across = lax.broadcasted_iota(jnp.int32, square, 1)
    ones = jnp.ones(square, BF16)
    code_row = tile * row_blocks
    for part in range(row_blocks):
        five = codes[pl.ds(code_row + part, 1), :]
        five = jnp.where(down == across, jnp.broadcast_to(five, square), 0).astype(F32)
        three_row = code_row + SPAN // LANES + rep + part
        three = jnp.concatenate(
            [codes[pl.ds(three_row, 1), :], codes[pl.ds(three_row + 1, 1), :]], 1
        ).astype(F32)
        step = staircase(three, -1)
        three = jnp.concatenate(
            [pltpu.roll(step, (-8 * group) % (2 * LANES), 1)[:, :LANES] for group in range(16)], 0
        )
        code = dot((4.0 * five).astype(BF16), ones) + three
        stack_value = jnp.zeros(square, F32)
        hairpin_value = jnp.zeros(square, F32)
        for first in range(4):
            for second in range(4):
                match = code == float(4 * first + second)
                stack_value = jnp.where(match, stack_ref[first, second], stack_value)
                hairpin_value = jnp.where(match, hairpin_ref[first, second], hairpin_value)
        at = slice(part * LANES, (part + 1) * LANES)
        interior[at] = (allowed[at].astype(F32) * stack_value) * (hairpin_value + interior[at])

    for block in range(1, reps):
        work_block(block, 0) if block < reps - 1 else None
        if block == 1:
            store_paired = pltpu.make_async_copy(interior, paired_hbm, local_sem.at[5])
            store_paired.start()
        if block < reps - 1:
            sum_copy(block).start()
    work_block(reps - 1, 0)

    for block in range(reps - 1):
        sum_copy(block).wait_recv()
    sums[reps - 1] = (sums[reps - 1] + others[0]) + (others[1] + others[2])
    store_split = pltpu.make_async_copy(sums.at[reps - 1], split_hbm, local_sem.at[6])
    store_split.start()
    store_paired.wait()
    store_split.wait()
    rim_copy.wait_send()
    wait_for(1, panel_count - 1, slice(None), panel_send)
    sent = sums.at[0 : reps - 1]
    pltpu.make_async_copy(sent, sent, sum_send).wait()


def hand_on(paired_in, split_in, paired_out, split_out, held, in_sem, out_sem):
    count = held.shape[1]
    size = held.shape[2]

    def ways(which, piece):
        source, target = ((paired_in, paired_out), (split_in, split_out))[which]
        at = pl.ds(piece * size, size)
        here = held.at[which, piece]
        return (
            pltpu.make_async_copy(source.at[at], here, in_sem.at[which, piece]),
            pltpu.make_async_copy(here, target.at[at], out_sem),
        )

    places = [(which, piece) for which in range(2) for piece in range(count)]
    for place in places:
        ways(*place)[0].start()
    for place in places:
        fetch, store = ways(*place)
        fetch.wait()
        store.start()
    pltpu.make_async_copy(held, held, out_sem).wait()


def on_device(
    tiles,
    reps,
    sequence_codes,
    pair_allowed,
    stack_weight,
    hairpin_weight,
    loop_weight,
    inner_pairs,
    multi_left,
    branch_right,
):
    row_count, cols_local = pair_allowed.shape
    panel_count = multi_left.shape[1]
    codes = sequence_codes.reshape(-1, LANES)
    inner = inner_pairs.T
    left = multi_left.reshape(row_count * panel_count, cols_local)
    right = branch_right[0]
    out = jax.ShapeDtypeStruct((row_count, cols_local), F32)
    any_space = pl.BlockSpec(memory_space=pl.ANY)
    smem = pl.BlockSpec(memory_space=pltpu.SMEM)
    vmem = pl.BlockSpec(memory_space=pltpu.VMEM)
    block = (row_count, LANES)
    pairs = (panel_count // 2, row_count, 2 * LANES)
    dma = pltpu.SemaphoreType.DMA
    results = pl.pallas_call(
        functools.partial(kernel, tiles, reps),
        out_shape=(out, out),
        in_specs=[smem, smem, vmem] + [any_space] * 5,
        out_specs=(any_space, any_space),
        scratch_shapes=[
            pltpu.VMEM(codes.shape, jnp.int32),
            pltpu.VMEM(block, jnp.int32),
            pltpu.VMEM(inner.shape, F32),
            pltpu.VMEM((row_count + RIM, 2 * LANES), F32),
            pltpu.VMEM((row_count + RIM, 2 * LANES), F32),
            pltpu.VMEM((32, LANES), F32),
            pltpu.VMEM(block, F32),
            pltpu.VMEM(left.shape, F32),
            pltpu.VMEM(pairs, BF16),
            pltpu.VMEM(pairs, BF16),
            pltpu.VMEM(right.shape, F32),
            pltpu.VMEM((reps,) + block, F32),
            pltpu.VMEM((reps - 1,) + block, F32),
            dma((7,)),
            dma,
            dma((panel_count // 2, reps)),
            dma,
            dma,
            dma,
            dma((reps - 1,)),
        ],
        compiler_params=pltpu.CompilerParams(
            collective_id=0, has_side_effects=True, vmem_limit_bytes=60 << 20
        ),
    )(stack_weight, hairpin_weight, loop_weight, codes, pair_allowed, inner, left, right)
    return pl.pallas_call(
        hand_on,
        out_shape=(out, out),
        in_specs=[any_space] * 2,
        out_specs=(any_space, any_space),
        scratch_shapes=[
            pltpu.VMEM((2, PIECES, row_count // PIECES, cols_local), F32),
            dma((2, PIECES)),
            dma,
        ],
        compiler_params=pltpu.CompilerParams(vmem_limit_bytes=60 << 20),
    )(*results)


def solution(mesh):
    placed = (
        P(),
        P("tile", "rep"),
        P(),
        P(),
        P(),
        P("tile", None),
        P("tile", None, "rep"),
        P("tile", None, "rep", None),
    )
    return jax.shard_map(
        functools.partial(on_device, mesh.shape["tile"], mesh.shape["rep"]),
        mesh=mesh,
        in_specs=placed,
        out_specs=(P("tile", "rep"), P("tile", "rep")),
        check_vma=False,
    )
```

```python
import functools

import jax
import jax.numpy as jnp
from jax import lax
from jax.experimental import pallas as pl
from jax.experimental.pallas import tpu as pltpu
from jax.sharding import PartitionSpec as P

LOOP = 30
SPAN = 8192
LANES = 128
PIECES = 2
RIM = 32
MESH = pl.DeviceIdType.MESH
F32 = jnp.float32
BF16 = jnp.bfloat16
BLOCK_ORDER = (2, 1, 3, 0)
SEND_ORDER = (2, 14, 4, 12, 6, 10, 8, 1, 15, 3, 13, 5, 11, 7, 9)


def halves(value):
    high = value.astype(BF16)
    return high, (value - high.astype(F32)).astype(BF16)


def dot(left, right):
    return jnp.dot(left, right, preferred_element_type=F32)


def product(left_high, left_low, right):
    right_high, right_low = halves(right)
    width = right.shape[1]
    both = dot(left_high, jnp.concatenate([right_high, right_low], 1))
    return both[:, :width] + both[:, width:] + dot(left_low, right_high)


def kernel(
    tiles,
    reps,
    stack_hbm,
    hairpin_hbm,
    loop_hbm,
    codes_hbm,
    allowed_hbm,
    inner_hbm,
    left_hbm,
    right_hbm,
    paired_hbm,
    split_hbm,
    codes,
    allowed,
    inner,
    rows,
    moving,
    weights,
    interior,
    left,
    left_high,
    left_low,
    panels,
    sums,
    others,
    local_sem,
    panel_send,
    panel_recv,
    rim_send,
    rim_recv,
    sum_send,
    sum_recv,
    stack_ref,
    hairpin_ref,
    loop_ref,
):
    tile = lax.axis_index("tile")
    rep = lax.axis_index("rep")
    panel_count, depth, _ = panels.shape
    row_count = rows.shape[0] - RIM

    def tile_at(step):
        return lax.rem(tile + step + tiles, tiles)

    def rep_at(step):
        return lax.rem(rep + step + reps, reps)

    barrier = pltpu.get_barrier_semaphore()

    @pl.loop(1, panel_count)
    def _(distance):
        pl.semaphore_signal(
            barrier, inc=1, device_id={"tile": tile_at(distance)}, device_id_type=MESH
        )

    for step in range(1, reps):
        pl.semaphore_signal(barrier, inc=1, device_id={"rep": rep_at(step)}, device_id_type=MESH)

    fetch_inner = pltpu.make_async_copy(inner_hbm, inner, local_sem.at[0])
    fetch_left = pltpu.make_async_copy(left_hbm, left, local_sem.at[1])
    fetch_right = pltpu.make_async_copy(right_hbm.at[0], panels.at[0], local_sem.at[2])
    fetch_codes = pltpu.make_async_copy(codes_hbm, codes, local_sem.at[3])
    fetch_allowed = pltpu.make_async_copy(allowed_hbm, allowed, local_sem.at[4])
    fetch_inner.start()
    fetch_left.start()
    fetch_right.start()
    fetch_codes.start()
    fetch_allowed.start()
    small = ((stack_hbm, stack_ref), (hairpin_hbm, hairpin_ref), (loop_hbm, loop_ref))
    fetch_small = [
        pltpu.make_async_copy(source, target, local_sem.at[7 + at])
        for at, (source, target) in enumerate(small)
    ]
    for fetch in fetch_small:
        fetch.start()
    pl.semaphore_wait(barrier, panel_count - 1 + reps - 1)

    def columns(block):
        start = rep_at(BLOCK_ORDER[block]) * LANES
        return pl.ds(pl.multiple_of(start, LANES), LANES)

    def panel_copy(distance, block):
        place = (distance, slice(None), columns(block))
        return pltpu.make_async_remote_copy(
            src_ref=right_hbm.at[place],
            dst_ref=panels.at[place],
            send_sem=panel_send,
            recv_sem=panel_recv.at[distance // 2, block],
            device_id={"tile": tile_at(-distance)},
            device_id_type=MESH,
        )

    def send_block(block):
        for distance in SEND_ORDER if block < reps - 1 else range(1, panel_count):
            panel_copy(distance, block).start()

    send_block(0)

    fetch_inner.wait()
    main_part = inner[pl.ds(pl.multiple_of(rep * LANES, LANES), LANES), :]
    rows[0:row_count, 0:LANES] = main_part.T
    tail_part = inner[pl.ds(pl.multiple_of((rep + 1) * LANES - 8, 8), LOOP + 8), :]
    rows[0:row_count, LANES : 2 * LANES] = jnp.zeros((row_count, LANES), F32)
    rows[0:row_count, LANES : LANES + LOOP + 8] = tail_part.T

    fetch_left.wait()
    own_row = lax.broadcasted_iota(jnp.int32, (row_count, LANES), 0)
    own_lane = lax.broadcasted_iota(jnp.int32, (row_count, LANES), 1)
    for panel in range(panel_count):
        value = left[pl.ds(panel, row_count, stride=panel_count), :]
        if panel == 0:
            value = jnp.where(own_lane + rep * LANES > own_row, value, 0.0)
        high, low = halves(value)
        at = slice((panel % 2) * LANES, (panel % 2 + 1) * LANES)
        left_high[panel // 2, :, at] = high
        left_low[panel // 2, :, at] = low

    rim_copy = pltpu.make_async_remote_copy(
        src_ref=rows.at[0:RIM],
        dst_ref=rows.at[row_count : row_count + RIM],
        send_sem=rim_send,
        recv_sem=rim_recv,
        device_id={"tile": tile_at(-1)},
        device_id_type=MESH,
    )
    rim_copy.start()
    for block in range(1, reps):
        send_block(block)
    fetch_right.wait()

    def wait_for(first, count, place, sem):
        ref = panels.at[pl.ds(first, count), :, place]
        pltpu.make_async_copy(ref, ref, sem).wait()

    def add_pair(block, pair):
        @pl.when(pair > 0)
        def _():
            wait_for(2 * pair, 2, columns(block), panel_recv.at[pair, block])

        @pl.when(pair == 0)
        def _():
            wait_for(1, 1, columns(block), panel_recv.at[pair, block])

        right = panels[pl.ds(2 * pair, 2), :, columns(block)].reshape(2 * depth, LANES)
        value = product(left_high[pair], left_low[pair], right)

        @pl.when(pair == 0)
        def _():
            sums[block] = value

        @pl.when(pair > 0)
        def _():
            sums[block] += value

    def sum_copy(block):
        step = BLOCK_ORDER[block]
        return pltpu.make_async_remote_copy(
            src_ref=sums.at[block],
            dst_ref=others.at[block],
            send_sem=sum_send,
            recv_sem=sum_recv.at[block],
            device_id={"rep": rep_at(step)},
            device_id_type=MESH,
        )

    def work_block(block, first):
        @pl.loop(first, panel_count // 2)
        def _(pair):
            add_pair(block, pair)

    work_block(0, 0)

    rim_copy.wait_recv()

    @pl.when(tile == tiles - 1)
    def _():
        rows[row_count : row_count + RIM, :] = jnp.zeros((RIM, 2 * LANES), F32)

    sum_copy(0).start()
    for fetch in fetch_small:
        fetch.wait()
    weights[...] = jnp.zeros_like(weights)
    weights[0 : LOOP + 1, 0 : LOOP + 1] = loop_ref[...]
    interior[...] = jnp.zeros_like(interior)

    moving[...] = rows[...]

    def staircase(row, direction):
        width = row.shape[1]
        step = jnp.broadcast_to(row, (8, width))
        down = lax.broadcasted_iota(jnp.int32, (8, width), 0)
        for bit in (1, 2, 4):
            step = jnp.where(down & bit != 0, pltpu.roll(step, (direction * bit) % width, 1), step)
        return step

    tall = (LANES + 40, LANES)
    source = lax.broadcasted_iota(jnp.int32, tall, 0)
    source = jnp.where(source < LANES, source, source - 8)
    behind = source - lax.broadcasted_iota(jnp.int32, tall, 1)
    behind = jnp.where(lax.broadcasted_iota(jnp.int32, tall, 0) // 8 == LANES // 8, -1, behind)
    groups = [group % 16 for group in (*range(16), *range(15, 20))]

    @pl.loop(1, LOOP + 2)
    def _(offset):
        row = pltpu.roll(weights[pl.ds(offset - 1, 1), :], LANES - LOOP - 1 + offset, 1)
        step = staircase(row, 1)
        bands = jnp.concatenate([pltpu.roll(step, 8 * group, 1) for group in groups], 0)
        bands = jnp.where((behind >= 0) & (behind <= LOOP + 1 - offset), bands, 0.0)
        bands = jnp.concatenate([bands, jnp.zeros((LANES - 40, LANES), F32)], 0)
        later = moving[1 : row_count + RIM, :]
        moving[0 : row_count + RIM - 1, :] = later
        high, low = halves(later[0:row_count])
        interior[...] += product(high, low, bands)

    fetch_codes.wait()
    fetch_allowed.wait()
    row_blocks = row_count // LANES
    square = (LANES, LANES)
    down = lax.broadcasted_iota(jnp.int32, square, 0)
    across = lax.broadcasted_iota(jnp.int32, square, 1)
    ones = jnp.ones(square, BF16)
    code_row = tile * row_blocks
    for part in range(row_blocks):
        five = codes[pl.ds(code_row + part, 1), :]
        five = jnp.where(down == across, jnp.broadcast_to(five, square), 0).astype(F32)
        three_row = code_row + SPAN // LANES + rep + part
        three = jnp.concatenate(
            [codes[pl.ds(three_row, 1), :], codes[pl.ds(three_row + 1, 1), :]], 1
        ).astype(F32)
        step = staircase(three, -1)
        three = jnp.concatenate(
            [pltpu.roll(step, (-8 * group) % (2 * LANES), 1)[:, :LANES] for group in range(16)], 0
        )
        code = dot((4.0 * five).astype(BF16), ones) + three
        stack_value = jnp.zeros(square, F32)
        hairpin_value = jnp.zeros(square, F32)
        for first in range(4):
            for second in range(4):
                match = code == float(4 * first + second)
                stack_value = jnp.where(match, stack_ref[first, second], stack_value)
                hairpin_value = jnp.where(match, hairpin_ref[first, second], hairpin_value)
        at = slice(part * LANES, (part + 1) * LANES)
        interior[at] = (allowed[at].astype(F32) * stack_value) * (hairpin_value + interior[at])

    for block in range(1, reps):
        work_block(block, 0) if block < reps - 1 else None
        if block == 1:
            store_paired = pltpu.make_async_copy(interior, paired_hbm, local_sem.at[5])
            store_paired.start()
        if block < reps - 1:
            sum_copy(block).start()
    work_block(reps - 1, 0)

    for block in range(reps - 1):
        sum_copy(block).wait_recv()
    sums[reps - 1] = (sums[reps - 1] + others[0]) + (others[1] + others[2])
    store_split = pltpu.make_async_copy(sums.at[reps - 1], split_hbm, local_sem.at[6])
    store_split.start()
    store_paired.wait()
    store_split.wait()
    rim_copy.wait_send()
    wait_for(1, panel_count - 1, slice(None), panel_send)
    sent = sums.at[0 : reps - 1]
    pltpu.make_async_copy(sent, sent, sum_send).wait()


def hand_on(paired_in, split_in, paired_out, split_out, out_sem):
    copies = [
        pltpu.make_async_copy(paired_in, paired_out, out_sem.at[0]),
        pltpu.make_async_copy(split_in, split_out, out_sem.at[1]),
    ]
    for copy in copies:
        copy.start()
    for copy in copies:
        copy.wait()


def on_device(
    tiles,
    reps,
    sequence_codes,
    pair_allowed,
    stack_weight,
    hairpin_weight,
    loop_weight,
    inner_pairs,
    multi_left,
    branch_right,
):
    row_count, cols_local = pair_allowed.shape
    panel_count = multi_left.shape[1]
    codes = sequence_codes.reshape(-1, LANES)
    inner = inner_pairs.T
    left = multi_left.reshape(row_count * panel_count, cols_local)
    right = branch_right[0]
    out = jax.ShapeDtypeStruct((row_count, cols_local), F32)
    any_space = pl.BlockSpec(memory_space=pl.ANY)
    block = (row_count, LANES)
    pairs = (panel_count // 2, row_count, 2 * LANES)
    dma = pltpu.SemaphoreType.DMA
    results = pl.pallas_call(
        functools.partial(kernel, tiles, reps),
        out_shape=(out, out),
        in_specs=[any_space] * 8,
        out_specs=(any_space, any_space),
        scratch_shapes=[
            pltpu.VMEM(codes.shape, jnp.int32),
            pltpu.VMEM(block, jnp.int32),
            pltpu.VMEM(inner.shape, F32),
            pltpu.VMEM((row_count + RIM, 2 * LANES), F32),
            pltpu.VMEM((row_count + RIM, 2 * LANES), F32),
            pltpu.VMEM((32, LANES), F32),
            pltpu.VMEM(block, F32),
            pltpu.VMEM(left.shape, F32),
            pltpu.VMEM(pairs, BF16),
            pltpu.VMEM(pairs, BF16),
            pltpu.VMEM(right.shape, F32),
            pltpu.VMEM((reps,) + block, F32),
            pltpu.VMEM((reps - 1,) + block, F32),
            dma((10,)),
            dma,
            dma((panel_count // 2, reps)),
            dma,
            dma,
            dma,
            dma((reps - 1,)),
            pltpu.SMEM(stack_weight.shape, F32),
            pltpu.SMEM(hairpin_weight.shape, F32),
            pltpu.VMEM(loop_weight.shape, F32),
        ],
        compiler_params=pltpu.CompilerParams(
            collective_id=0, has_side_effects=True, vmem_limit_bytes=53 << 20
        ),
    )(*[pltpu.with_memory_space_constraint(x, pltpu.HBM) for x in (stack_weight, hairpin_weight, loop_weight, codes, pair_allowed, inner, left, right)])
    return pl.pallas_call(
        hand_on,
        out_shape=(out, out),
        in_specs=[any_space] * 2,
        out_specs=(any_space, any_space),
        scratch_shapes=[
            dma((2,)),
        ],
        compiler_params=pltpu.CompilerParams(vmem_limit_bytes=16 << 20),
    )(*results)


def solution(mesh):
    placed = (
        P(),
        P("tile", "rep"),
        P(),
        P(),
        P(),
        P("tile", None),
        P("tile", None, "rep"),
        P("tile", None, "rep", None),
    )
    return jax.shard_map(
        functools.partial(on_device, mesh.shape["tile"], mesh.shape["rep"]),
        mesh=mesh,
        in_specs=placed,
        out_specs=(P("tile", "rep"), P("tile", "rep")),
        check_vma=False,
    )
```

```python
import functools

import jax
import jax.numpy as jnp
from jax import lax
from jax.experimental import pallas as pl
from jax.experimental.pallas import tpu as pltpu
from jax.sharding import PartitionSpec as P

LOOP = 30
SPAN = 8192
LANES = 128
PIECES = 2
RIM = 32
MESH = pl.DeviceIdType.MESH
F32 = jnp.float32
BF16 = jnp.bfloat16
BLOCK_ORDER = (2, 1, 3, 0)
SEND_ORDER = (2, 14, 4, 12, 6, 10, 8, 1, 15, 3, 13, 5, 11, 7, 9)


def halves(value):
    high = value.astype(BF16)
    return high, (value - high.astype(F32)).astype(BF16)


def dot(left, right):
    return jnp.dot(left, right, preferred_element_type=F32)


def product(left_high, left_low, right):
    right_high, right_low = halves(right)
    width = right.shape[1]
    both = dot(left_high, jnp.concatenate([right_high, right_low], 1))
    return both[:, :width] + both[:, width:] + dot(left_low, right_high)


def kernel(
    tiles,
    reps,
    stack_hbm,
    hairpin_hbm,
    loop_hbm,
    codes_hbm,
    allowed_hbm,
    inner_hbm,
    left_hbm,
    right_hbm,
    paired_hbm,
    split_hbm,
    codes,
    allowed,
    inner,
    rows,
    moving,
    weights,
    interior,
    left,
    left_high,
    left_low,
    panels,
    sums,
    others,
    local_sem,
    panel_send,
    panel_recv,
    rim_send,
    rim_recv,
    sum_send,
    sum_recv,
    stack_ref,
    hairpin_ref,
    loop_ref,
):
    tile = lax.axis_index("tile")
    rep = lax.axis_index("rep")
    panel_count, depth, _ = panels.shape
    row_count = rows.shape[0] - RIM

    def tile_at(step):
        return lax.rem(tile + step + tiles, tiles)

    def rep_at(step):
        return lax.rem(rep + step + reps, reps)

    barrier = pltpu.get_barrier_semaphore()

    @pl.loop(1, panel_count)
    def _(distance):
        pl.semaphore_signal(
            barrier, inc=1, device_id={"tile": tile_at(distance)}, device_id_type=MESH
        )

    for step in range(1, reps):
        pl.semaphore_signal(barrier, inc=1, device_id={"rep": rep_at(step)}, device_id_type=MESH)

    fetch_inner = pltpu.make_async_copy(inner_hbm, inner, local_sem.at[0])
    fetch_left = pltpu.make_async_copy(left_hbm, left, local_sem.at[1])
    fetch_right = pltpu.make_async_copy(right_hbm.at[0], panels.at[0], local_sem.at[2])
    fetch_codes = pltpu.make_async_copy(codes_hbm, codes, local_sem.at[3])
    fetch_allowed = pltpu.make_async_copy(allowed_hbm, allowed, local_sem.at[4])
    fetch_inner.start()
    fetch_left.start()
    fetch_right.start()
    fetch_codes.start()
    fetch_allowed.start()
    small = ((stack_hbm, stack_ref), (hairpin_hbm, hairpin_ref), (loop_hbm, loop_ref))
    fetch_small = [
        pltpu.make_async_copy(source, target, local_sem.at[7 + at])
        for at, (source, target) in enumerate(small)
    ]
    for fetch in fetch_small:
        fetch.start()
    pl.semaphore_wait(barrier, panel_count - 1 + reps - 1)

    def columns(block):
        start = rep_at(BLOCK_ORDER[block]) * LANES
        return pl.ds(pl.multiple_of(start, LANES), LANES)

    def panel_copy(distance, block):
        place = (distance, slice(None), columns(block))
        return pltpu.make_async_remote_copy(
            src_ref=right_hbm.at[place],
            dst_ref=panels.at[place],
            send_sem=panel_send,
            recv_sem=panel_recv.at[distance // 2, block],
            device_id={"tile": tile_at(-distance)},
            device_id_type=MESH,
        )

    def send_block(block):
        for distance in SEND_ORDER if block < reps - 1 else range(1, panel_count):
            panel_copy(distance, block).start()

    send_block(0)

    fetch_inner.wait()
    main_part = inner[pl.ds(pl.multiple_of(rep * LANES, LANES), LANES), :]
    rows[0:row_count, 0:LANES] = main_part.T
    tail_part = inner[pl.ds(pl.multiple_of((rep + 1) * LANES - 8, 8), LOOP + 8), :]
    rows[0:row_count, LANES : 2 * LANES] = jnp.zeros((row_count, LANES), F32)
    rows[0:row_count, LANES : LANES + LOOP + 8] = tail_part.T

    fetch_left.wait()
    own_row = lax.broadcasted_iota(jnp.int32, (row_count, LANES), 0)
    own_lane = lax.broadcasted_iota(jnp.int32, (row_count, LANES), 1)
    for panel in range(panel_count):
        value = left[pl.ds(panel, row_count, stride=panel_count), :]
        if panel == 0:
            value = jnp.where(own_lane + rep * LANES > own_row, value, 0.0)
        high, low = halves(value)
        at = slice((panel % 2) * LANES, (panel % 2 + 1) * LANES)
        left_high[panel // 2, :, at] = high
        left_low[panel // 2, :, at] = low

    rim_copy = pltpu.make_async_remote_copy(
        src_ref=rows.at[0:RIM],
        dst_ref=rows.at[row_count : row_count + RIM],
        send_sem=rim_send,
        recv_sem=rim_recv,
        device_id={"tile": tile_at(-1)},
        device_id_type=MESH,
    )
    rim_copy.start()
    for block in range(1, reps):
        send_block(block)
    fetch_right.wait()

    def wait_for(first, count, place, sem):
        ref = panels.at[pl.ds(first, count), :, place]
        pltpu.make_async_copy(ref, ref, sem).wait()

    def add_pair(block, pair):
        @pl.when(pair > 0)
        def _():
            wait_for(2 * pair, 2, columns(block), panel_recv.at[pair, block])

        @pl.when(pair == 0)
        def _():
            wait_for(1, 1, columns(block), panel_recv.at[pair, block])

        right = panels[pl.ds(2 * pair, 2), :, columns(block)].reshape(2 * depth, LANES)
        value = product(left_high[pair], left_low[pair], right)

        @pl.when(pair == 0)
        def _():
            sums[block] = value

        @pl.when(pair > 0)
        def _():
            sums[block] += value

    def sum_copy(block):
        step = BLOCK_ORDER[block]
        return pltpu.make_async_remote_copy(
            src_ref=sums.at[block],
            dst_ref=others.at[block],
            send_sem=sum_send,
            recv_sem=sum_recv.at[block],
            device_id={"rep": rep_at(step)},
            device_id_type=MESH,
        )

    def work_block(block, first):
        @pl.loop(first, panel_count // 2)
        def _(pair):
            add_pair(block, pair)

    work_block(0, 0)

    rim_copy.wait_recv()

    @pl.when(tile == tiles - 1)
    def _():
        rows[row_count : row_count + RIM, :] = jnp.zeros((RIM, 2 * LANES), F32)

    sum_copy(0).start()
    for fetch in fetch_small:
        fetch.wait()
    weights[...] = jnp.zeros_like(weights)
    weights[0 : LOOP + 1, 0 : LOOP + 1] = loop_ref[...]
    interior[...] = jnp.zeros_like(interior)

    moving[...] = rows[...]

    def staircase(row, direction):
        width = row.shape[1]
        step = jnp.broadcast_to(row, (8, width))
        down = lax.broadcasted_iota(jnp.int32, (8, width), 0)
        for bit in (1, 2, 4):
            step = jnp.where(down & bit != 0, pltpu.roll(step, (direction * bit) % width, 1), step)
        return step

    tall = (LANES + 40, LANES)
    source = lax.broadcasted_iota(jnp.int32, tall, 0)
    source = jnp.where(source < LANES, source, source - 8)
    behind = source - lax.broadcasted_iota(jnp.int32, tall, 1)
    behind = jnp.where(lax.broadcasted_iota(jnp.int32, tall, 0) // 8 == LANES // 8, -1, behind)
    groups = [group % 16 for group in (*range(16), *range(15, 20))]

    @pl.loop(1, LOOP + 2)
    def _(offset):
        row = pltpu.roll(weights[pl.ds(offset - 1, 1), :], LANES - LOOP - 1 + offset, 1)
        step = staircase(row, 1)
        bands = jnp.concatenate([pltpu.roll(step, 8 * group, 1) for group in groups], 0)
        bands = jnp.where((behind >= 0) & (behind <= LOOP + 1 - offset), bands, 0.0)
        bands = jnp.concatenate([bands, jnp.zeros((LANES - 40, LANES), F32)], 0)
        later = moving[1 : row_count + RIM, :]
        moving[0 : row_count + RIM - 1, :] = later
        high, low = halves(later[0:row_count])
        interior[...] += product(high, low, bands)

    fetch_codes.wait()
    fetch_allowed.wait()
    row_blocks = row_count // LANES
    square = (LANES, LANES)
    down = lax.broadcasted_iota(jnp.int32, square, 0)
    across = lax.broadcasted_iota(jnp.int32, square, 1)
    ones = jnp.ones(square, BF16)
    code_row = tile * row_blocks
    for part in range(row_blocks):
        five = codes[pl.ds(code_row + part, 1), :]
        five = jnp.where(down == across, jnp.broadcast_to(five, square), 0).astype(F32)
        three_row = code_row + SPAN // LANES + rep + part
        three = jnp.concatenate(
            [codes[pl.ds(three_row, 1), :], codes[pl.ds(three_row + 1, 1), :]], 1
        ).astype(F32)
        step = staircase(three, -1)
        three = jnp.concatenate(
            [pltpu.roll(step, (-8 * group) % (2 * LANES), 1)[:, :LANES] for group in range(16)], 0
        )
        code = dot((4.0 * five).astype(BF16), ones) + three
        stack_value = jnp.zeros(square, F32)
        hairpin_value = jnp.zeros(square, F32)
        for first in range(4):
            for second in range(4):
                match = code == float(4 * first + second)
                stack_value = jnp.where(match, stack_ref[first, second], stack_value)
                hairpin_value = jnp.where(match, hairpin_ref[first, second], hairpin_value)
        at = slice(part * LANES, (part + 1) * LANES)
        interior[at] = (allowed[at].astype(F32) * stack_value) * (hairpin_value + interior[at])

    for block in range(1, reps):
        work_block(block, 0) if block < reps - 1 else None
        if block == 1:
            store_paired = pltpu.make_async_copy(interior, paired_hbm, local_sem.at[5])
            store_paired.start()
        if block < reps - 1:
            sum_copy(block).start()
    work_block(reps - 1, 0)

    for block in range(reps - 1):
        sum_copy(block).wait_recv()
    own = sums.at[reps - 1]
    half = row_count // 2
    for part in range(2):
        at = slice(part * half, (part + 1) * half)
        own[at] = (own[at] + others[0, at]) + (others[1, at] + others[2, at])
        pltpu.make_async_copy(own.at[at], split_hbm.at[at], local_sem.at[6]).start()
    store_split = pltpu.make_async_copy(own, split_hbm, local_sem.at[6])
    store_paired.wait()
    store_split.wait()
    rim_copy.wait_send()
    wait_for(1, panel_count - 1, slice(None), panel_send)
    sent = sums.at[0 : reps - 1]
    pltpu.make_async_copy(sent, sent, sum_send).wait()


def hand_on(paired_in, split_in, paired_out, split_out, out_sem):
    copies = [
        pltpu.make_async_copy(paired_in, paired_out, out_sem.at[0]),
        pltpu.make_async_copy(split_in, split_out, out_sem.at[1]),
    ]
    for copy in copies:
        copy.start()
    for copy in copies:
        copy.wait()


def on_device(
    tiles,
    reps,
    sequence_codes,
    pair_allowed,
    stack_weight,
    hairpin_weight,
    loop_weight,
    inner_pairs,
    multi_left,
    branch_right,
):
    row_count, cols_local = pair_allowed.shape
    panel_count = multi_left.shape[1]
    codes = sequence_codes.reshape(-1, LANES)
    inner = inner_pairs.T
    left = multi_left.reshape(row_count * panel_count, cols_local)
    right = branch_right[0]
    out = jax.ShapeDtypeStruct((row_count, cols_local), F32)
    any_space = pl.BlockSpec(memory_space=pl.ANY)
    block = (row_count, LANES)
    pairs = (panel_count // 2, row_count, 2 * LANES)
    dma = pltpu.SemaphoreType.DMA
    results = pl.pallas_call(
        functools.partial(kernel, tiles, reps),
        out_shape=(out, out),
        in_specs=[any_space] * 8,
        out_specs=(any_space, any_space),
        scratch_shapes=[
            pltpu.VMEM(codes.shape, jnp.int32),
            pltpu.VMEM(block, jnp.int32),
            pltpu.VMEM(inner.shape, F32),
            pltpu.VMEM((row_count + RIM, 2 * LANES), F32),
            pltpu.VMEM((row_count + RIM, 2 * LANES), F32),
            pltpu.VMEM((32, LANES), F32),
            pltpu.VMEM(block, F32),
            pltpu.VMEM(left.shape, F32),
            pltpu.VMEM(pairs, BF16),
            pltpu.VMEM(pairs, BF16),
            pltpu.VMEM(right.shape, F32),
            pltpu.VMEM((reps,) + block, F32),
            pltpu.VMEM((reps - 1,) + block, F32),
            dma((10,)),
            dma,
            dma((panel_count // 2, reps)),
            dma,
            dma,
            dma,
            dma((reps - 1,)),
            pltpu.SMEM(stack_weight.shape, F32),
            pltpu.SMEM(hairpin_weight.shape, F32),
            pltpu.VMEM(loop_weight.shape, F32),
        ],
        compiler_params=pltpu.CompilerParams(
            collective_id=0, has_side_effects=True, vmem_limit_bytes=53 << 20
        ),
    )(*[pltpu.with_memory_space_constraint(x, pltpu.HBM) for x in (stack_weight, hairpin_weight, loop_weight, codes, pair_allowed, inner, left, right)])
    return pl.pallas_call(
        hand_on,
        out_shape=(out, out),
        in_specs=[any_space] * 2,
        out_specs=(any_space, any_space),
        scratch_shapes=[
            dma((2,)),
        ],
        compiler_params=pltpu.CompilerParams(vmem_limit_bytes=16 << 20),
    )(*results)


def solution(mesh):
    placed = (
        P(),
        P("tile", "rep"),
        P(),
        P(),
        P(),
        P("tile", None),
        P("tile", None, "rep"),
        P("tile", None, "rep", None),
    )
    return jax.shard_map(
        functools.partial(on_device, mesh.shape["tile"], mesh.shape["rep"]),
        mesh=mesh,
        in_specs=placed,
        out_specs=(P("tile", "rep"), P("tile", "rep")),
        check_vma=False,
    )
```
